32 devices in a mesh: wide: 8 (over y, x, core), narrow: 4 (over z).
Axes of the slice: x: 2, y: 2, z: 4, core: 2. Of those that a mesh axis runs over, the one named last changes fastest.
Arguments:
- tokens: bfloat16 [4096, 4096], P(('wide', 'narrow')), may hold values from -6 to 6
- cotangent: bfloat16 [4096, 4096], P(('wide', 'narrow')), may hold values from -6 to 6
- weights: bfloat16 [32, 6, 256, 256], P(('wide', 'narrow')), may hold values from -0.1875 to 0.1875
- block_index: int32 [32, 6], P(('wide', 'narrow')), may hold values from 0 to 15, as said below
- block_counts: int32 [32], P(('wide', 'narrow')), may hold values from 1 to 6, as said below
Outputs:
- mixed: bfloat16 [4096, 4096], P(('wide', 'narrow'))
- grad_tokens: bfloat16 [4096, 4096], P(('wide', 'narrow'))
The draws below stay inside these ranges and needn't reach their ends.
Inputs may be any that keep to these rules, and one draw needn't show every extreme that they name: `block_index`: each row lists 6 distinct blocks. `block_counts`: slots at or beyond a row's count are unused.
All inputs are finite; a program needn't handle non-finite values.
Results may differ from the reference program's by a relative error of at most 0.008.
Values may be sent and summed in bfloat16 or wider, within the bound.
No kernel may reach another device: no remote copies, remote signals or barrier semaphores. Data moves between devices by JAX's collectives and lax.ppermute only.
A program may use at most 192 MiB of HBM per device.

```python
import jax
import jax.numpy as jnp
from jax import lax

D = 4096
BLOCK = 256
KB = 6
PANELS = 16
TOKENS = 4096
N_NARROW = 4


def draw_block_index(key, part):
    row_keys = jax.random.split(key, 2 * PANELS)

    def one_row(row_key):
        return jax.random.permutation(row_key, D // BLOCK)[:KB]
    return jax.vmap(one_row)(row_keys).astype(jnp.int32)


def draw_block_counts(key, part):
    base_counts = jax.random.randint(jax.random.fold_in(key, 1), (2 * PANELS,), 1, KB + 1)
    full_spot = jax.random.randint(jax.random.fold_in(key, 2), (), 0, 2 * PANELS)
    return base_counts.at[full_spot].set(KB).astype(jnp.int32)


def level_of(stream_key, dims, cuts, low, top_value):
    gain, own = 1.0, jax.random.fold_in(stream_key, 6)
    for axis_at, shards_of in cuts:
        heights = jnp.exp(jax.random.uniform(jax.random.fold_in(own, axis_at), (shards_of,), jnp.float32, low / len(cuts), top_value / len(cuts)))
        gain = gain * jnp.repeat(heights, dims[axis_at] // shards_of).reshape([-1 if axis == axis_at else 1 for axis in range(len(dims))])
    return gain


def scatter_about(own_key, extent, scale, most, cuts=(), held_as=jnp.bfloat16):
    array = scale * jax.random.normal(own_key, extent, jnp.float32)
    if cuts:
        array = array * level_of(own_key, extent, cuts, -0.22, 0.18)
    return jnp.clip(array, -most, most).astype(held_as)


def setup_inputs(seed: int = 0) -> dict:
    key_of = jax.random.split(jax.random.key(seed), 6)
    tokens = scatter_about(key_of[0], (TOKENS, D), 1.0, 6.0, ((0, 32),))
    cotangent = scatter_about(key_of[1], (TOKENS, D), 1.0, 6.0, ((0, 32),))
    weights = scatter_about(key_of[2], (2 * PANELS, KB, BLOCK, BLOCK), (D // 4) ** -0.5, 0.1875, ((0, 32),))
    block_index = draw_block_index(jax.random.fold_in(key_of[5], 71), 0)
    block_counts = draw_block_counts(jax.random.fold_in(key_of[5], 71), 0)
    return dict(tokens=tokens, cotangent=cotangent, weights=weights, block_index=block_index, block_counts=block_counts)


def activate(values):
    return jax.nn.gelu(values, approximate=True)

def reference(tokens, cotangent, weights, block_index, block_counts):
    num_rows = tokens.shape[0]
    num_blocks = D // BLOCK
    live_mask = (jnp.arange(KB)[None, :] < block_counts[:, None]).astype(jnp.bfloat16)
    kept_blocks = weights * live_mask[:, :, None, None]
    tok_blocks = tokens.reshape(num_rows, num_blocks, BLOCK).astype(jnp.float32)
    cot_blocks = cotangent.reshape(num_rows, num_blocks, BLOCK).astype(jnp.float32)

    def run_group(group_num):

        def one_panel(totals, step_num):
            out_acc, grad_acc = totals
            panel_num = step_num * N_NARROW + group_num
            w_first = lax.dynamic_index_in_dim(kept_blocks, panel_num, 0, keepdims=False).astype(jnp.float32)
            w_second = lax.dynamic_index_in_dim(kept_blocks, panel_num + PANELS, 0, keepdims=False).astype(jnp.float32)
            idx_first = lax.dynamic_index_in_dim(block_index, panel_num, 0, keepdims=False)
            idx_second = lax.dynamic_index_in_dim(block_index, panel_num + PANELS, 0, keepdims=False)
            picked = jnp.take(tok_blocks, idx_first, axis=1)
            pre_act = jnp.einsum('tjd,jdh->th', picked, w_first)
            act_out = activate(pre_act).astype(jnp.bfloat16).astype(jnp.float32)
            out_acc = out_acc.at[:, idx_second].add(jnp.einsum('th,jhd->tjd', act_out, w_second))
            cot_picked = jnp.take(cot_blocks, idx_second, axis=1)
            grad_act = jnp.einsum('tjd,jhd->th', cot_picked, w_second)
            grad_pre = jax.vjp(activate, pre_act)[1](grad_act)[0].astype(jnp.bfloat16).astype(jnp.float32)
            grad_acc = grad_acc.at[:, idx_first].add(jnp.einsum('th,jdh->tjd', grad_pre, w_first))
            return ((out_acc, grad_acc), None)
        zeros_acc = jnp.zeros((num_rows, num_blocks, BLOCK), jnp.float32)
        totals, _ = lax.scan(one_panel, (zeros_acc, zeros_acc), jnp.arange(PANELS // N_NARROW))
        return (totals[0].astype(jnp.bfloat16), totals[1].astype(jnp.bfloat16))

    def add_group(group_num, sums):
        part_y, part_x = run_group(group_num)
        return (sums[0] + part_y.astype(jnp.float32), sums[1] + part_x.astype(jnp.float32))
    zeros_sum = jnp.zeros((num_rows, num_blocks, BLOCK), jnp.float32)
    sum_y, sum_x = lax.fori_loop(0, N_NARROW, add_group, (zeros_sum, zeros_sum))
    mixed = sum_y.reshape(num_rows, D).astype(jnp.bfloat16)
    grad_tokens = sum_x.reshape(num_rows, D).astype(jnp.bfloat16)
    return (mixed, grad_tokens)
```

```python
import functools

import jax
import jax.numpy as jnp
from jax import lax
from jax.experimental import pallas as pl
from jax.experimental.pallas import tpu as pltpu
from jax.sharding import PartitionSpec as P

ROOT_2_OVER_PI = 0.7978845608028654
CUBIC = 0.044715
BOTH = ("wide", "narrow")
VMEM_LIMIT = 32 * 1024 * 1024
PAIRS_VMEM_LIMIT = 16 * 1024 * 1024

ENDS = [(0, 1), (1, 0), (2, 3), (3, 2)]
MIDDLE = [(1, 2), (2, 1)]
OUTWARD = [(1, 0), (2, 3)]


def gelu_and_slope(v):
    inner = ROOT_2_OVER_PI * (v + CUBIC * (v * v * v))
    t = jnp.tanh(inner)
    cdf = 0.5 * (1.0 + t)
    slope = cdf + (0.5 * v) * (1.0 - t * t) * (ROOT_2_OVER_PI * (1.0 + (3.0 * CUBIC) * (v * v)))
    return v * cdf, slope


def dot_plain(a, b):
    return lax.dot_general(a, b, (((1,), (0,)), ((), ())), preferred_element_type=jnp.float32)


def dot_turned(a, b):
    return lax.dot_general(a, b, (((1,), (1,)), ((), ())), preferred_element_type=jnp.float32)


def lanes(index, width):
    return pl.ds(pl.multiple_of(index * width, width), width)


def run_panel(meta, row1, row2, slots, width, toks, cots, w1, w2, out_accs, grad_accs):
    count1, count2 = meta[row1, slots], meta[row2, slots]

    def kept(parts, row, count, j):
        at = lanes(meta[row, j], width)
        value = jnp.concatenate([part[:, at] for part in parts], axis=0)
        return value if j == 0 else jnp.where(j < count, value, jnp.zeros_like(value))

    pre = dot_plain(kept(toks, row1, count1, 0), w1(0))
    gact = dot_turned(kept(cots, row2, count2, 0), w2(0))
    for j in range(1, slots):
        pre = pre + dot_plain(kept(toks, row1, count1, j), w1(j))
    for j in range(1, slots):
        gact = gact + dot_turned(kept(cots, row2, count2, j), w2(j))
    act, slope = gelu_and_slope(pre)
    act = act.astype(jnp.bfloat16)
    gpre = (gact * slope).astype(jnp.bfloat16)
    zero = jnp.zeros_like(act)

    def add(accs, block, value):
        at = 0
        for acc in accs:
            rows = acc.shape[0]
            acc[:, lanes(block, width)] += value[at : at + rows]
            at += rows

    for j in range(slots):
        add(out_accs, meta[row2, j], dot_plain(jnp.where(j < count2, act, zero), w2(j)))
    for j in range(slots):
        add(grad_accs, meta[row1, j], dot_turned(jnp.where(j < count1, gpre, zero), w1(j)))


def pairs_kernel(plan, *refs):
    pairs, spans, starts, rounds, slots, width = (
        plan["pairs"], plan["spans"], plan["starts"], plan["rounds"], plan["slots"], plan["width"],
    )
    n, parts = len(pairs), len(spans)
    refs = list(refs)

    def take(count):
        taken = refs[:count]
        del refs[:count]
        return taken

    pos, meta = take(2)
    fed = take(3 if starts else 2)
    held = [[take(k) for k in counts] for _, _, counts in pairs]
    if starts:
        tok, cot = take(2)
    else:
        tok, cot = fed
        take(2 * parts)
    sums = take(2 * parts)
    rounded = take(2 * parts if rounds else 0)
    blocks, block_sem = take(2)
    low, z = pos[0], pos[1]
    middle = (z == 1) | (z == 2)

    feeding = []
    if starts:
        own_tok, own_cot, other = fed
        rows = own_tok.shape[0]
        first, second = pl.ds(0, rows), pl.ds(rows, rows)
        feeding = [
            pltpu.make_async_copy(src, dst, refs[0].at[k])
            for k, (src, dst) in enumerate((
                (own_tok, tok.at[first]), (other.at[first], tok.at[second]),
                (own_cot, cot.at[first]), (other.at[second], cot.at[second]),
            ))
        ]
    for copy in feeding:
        copy.start()

    def block_copy(k, side, source):
        return pltpu.make_async_copy(source.at[0], blocks.at[k, side], block_sem.at[k, side])

    def begin(k, side):
        for which in range(2):
            choice = held[k][which]
            here = low == (1 if which == side else 0)
            for pick, source in enumerate(choice):
                wanted = here
                if len(choice) == 2:
                    wanted = here & (middle if pick == 0 else jnp.logical_not(middle))
                pl.when(wanted)(lambda source=source: block_copy(k, side, source).start())

    for k in range(n):
        begin(k, 0)
        begin(k, 1)
    if starts:
        for total in sums:
            total[...] = jnp.zeros_like(total)
    for copy in feeding:
        copy.wait()
    toks = [tok.at[pl.ds(at, size)] for at, size in spans]
    cots = [cot.at[pl.ds(at, size)] for at, size in spans]
    for k, (flip, kind, _) in enumerate(pairs):
        there = {
            "own": z,
            "near": z ^ 1,
            "third": jnp.where(z < 2, 2, 1),
            "last": jnp.where(z < 2, 3, 0),
        }[kind]
        for side in range(2):
            block_copy(k, side, held[k][side][0]).wait()
        at = (z ^ there) * 4 + 2 * flip
        run_panel(
            meta, at + 1 - low, at + low, slots, width, toks, cots,
            lambda j, k=k: blocks[k, 0, j], lambda j, k=k: blocks[k, 1, j],
            sums[:parts], sums[parts:],
        )
    for total, out in zip(sums, rounded):
        out[...] = total[...].astype(out.dtype)


def run_pairs(pos, meta, fed, items, spans, accs, rounds, sizes):
    slots, width = sizes
    parts, n = len(spans), len(items)
    starts = accs is None
    model = fed[0].shape[1]
    plan = dict(
        pairs=[(flip, kind, (len(first), len(second))) for flip, kind, first, second in items],
        spans=spans, starts=starts, rounds=rounds, slots=slots, width=width,
    )
    smem = pl.BlockSpec(memory_space=pltpu.SMEM)
    vmem = pl.BlockSpec(memory_space=pltpu.VMEM)
    hbm = pl.BlockSpec(memory_space=pl.ANY)

    def off_chip(value):
        return pltpu.with_memory_space_constraint(value, pltpu.HBM)

    blocks = [off_chip(a) for item in items for choice in item[2:] for a in choice]
    if starts:
        fed = [off_chip(value) for value in fed]
    operands = [pos, meta, *fed, *blocks, *(accs or [])]
    first_acc = len(operands) - 2 * parts
    out_shape = [jax.ShapeDtypeStruct((size, model), jnp.float32) for _, size in spans] * 2
    if rounds:
        out_shape += [jax.ShapeDtypeStruct((size, model), jnp.bfloat16) for _, size in spans] * 2
    rows = sum(size for _, size in spans)
    scratch = [pltpu.VMEM((n, 2, slots, width, width), jnp.bfloat16), pltpu.SemaphoreType.DMA((n, 2))]
    if starts:
        out_shape = [jax.ShapeDtypeStruct((rows, model), jnp.bfloat16)] * 2 + out_shape
        scratch += [pltpu.SemaphoreType.DMA((4,))]
    outs = pl.pallas_call(
        functools.partial(pairs_kernel, plan),
        out_shape=out_shape,
        in_specs=[smem, smem] + [hbm if starts else vmem] * len(fed) + [hbm] * len(blocks) + [vmem] * len(accs or []),
        out_specs=[vmem] * len(out_shape),
        scratch_shapes=scratch,
        input_output_aliases={} if starts else {first_acc + i: i for i in range(2 * parts)},
        compiler_params=pltpu.CompilerParams(vmem_limit_bytes=PAIRS_VMEM_LIMIT),
        cost_estimate=pl.CostEstimate(
            flops=n * 4 * slots * 2 * rows * width * width,
            transcendentals=n * rows * width,
            bytes_accessed=2 * n * slots * width * width * 2,
        ),
    )(*operands)
    return (outs[:2] if starts else fed), outs[-2 * parts :]


def all_panels_kernel(slots, width, half, meta, tok, cot, held, out, grad, blocks, out_acc, grad_acc, sem):
    def copies(p, buf):
        return [
            pltpu.make_async_copy(held.at[p], blocks.at[buf, 0], sem.at[buf, 0]),
            pltpu.make_async_copy(held.at[half + p], blocks.at[buf, 1], sem.at[buf, 1]),
        ]

    out_acc[...] = jnp.zeros_like(out_acc)
    grad_acc[...] = jnp.zeros_like(grad_acc)
    for copy in copies(0, 0):
        copy.start()

    def step(p, _):
        buf = lax.rem(p, 2)

        @pl.when(p + 1 < half)
        def _():
            for copy in copies(p + 1, 1 - buf):
                copy.start()

        for copy in copies(p, buf):
            copy.wait()
        run_panel(
            meta, p, half + p, slots, width, [tok], [cot],
            lambda j: blocks[buf, 0, j], lambda j: blocks[buf, 1, j], [out_acc], [grad_acc],
        )
        return 0

    lax.fori_loop(0, half, step, 0)
    out[...] = out_acc[...].astype(out.dtype)
    grad[...] = grad_acc[...].astype(grad.dtype)


def run_all(meta, tokens, cotangent, gathered):
    count, slots, width, _ = gathered.shape
    rows, model = tokens.shape
    vmem = pl.BlockSpec(memory_space=pltpu.VMEM)
    return pl.pallas_call(
        functools.partial(all_panels_kernel, slots, width, count // 2),
        out_shape=[jax.ShapeDtypeStruct((rows, model), jnp.bfloat16)] * 2,
        in_specs=[pl.BlockSpec(memory_space=pltpu.SMEM), vmem, vmem, pl.BlockSpec(memory_space=pl.ANY)],
        out_specs=[vmem] * 2,
        scratch_shapes=[
            pltpu.VMEM((2, 2, slots, width, width), jnp.bfloat16),
            pltpu.VMEM((rows, model), jnp.float32),
            pltpu.VMEM((rows, model), jnp.float32),
            pltpu.SemaphoreType.DMA((2, 2)),
        ],
        compiler_params=pltpu.CompilerParams(vmem_limit_bytes=VMEM_LIMIT),
    )(meta, tokens, cotangent, gathered)


def together(*values):
    return lax.optimization_barrier(values)


def exchange_plan(wide, narrow):
    return wide == 8 and narrow == 4


def body(tokens, cotangent, weights, block_index, block_counts):
    wide, narrow = lax.axis_size("wide"), lax.axis_size("narrow")
    slots, width = weights.shape[1], weights.shape[2]
    own_meta = jnp.concatenate([block_index, block_counts[:, None]], axis=1)
    if not exchange_plan(wide, narrow):
        meta = lax.all_gather(own_meta, BOTH, axis=0, tiled=True)
        gathered = lax.all_gather(weights, BOTH, axis=0, tiled=True)
        return tuple(run_all(meta, tokens, cotangent, gathered))

    def across(value, bit):
        return lax.ppermute(value, "wide", [(i, i ^ bit) for i in range(wide)])

    core, x, y = (functools.partial(across, bit=bit) for bit in (1, 2, 4))

    def line(value, pairs):
        return lax.ppermute(value, "narrow", pairs)

    w, z = lax.axis_index("wide"), lax.axis_index("narrow")
    pos = jnp.stack([(w < wide // 2).astype(jnp.int32), z.astype(jnp.int32)])
    mid = (z == 1) | (z == 2)
    run = functools.partial(run_pairs, sizes=(slots, width))

    def doubled(table, moved):
        return jnp.concatenate([table, moved], axis=0)

    own = weights
    x_own, y_own, near, beyond = x(own), y(own), line(own, ENDS), line(own, MIDDLE)
    meta = doubled(own_meta, y(own_meta))
    both = jnp.concatenate([tokens, cotangent], axis=0)

    x_own, y_own, near, beyond, meta, both = together(x_own, y_own, near, beyond, meta, both)
    x_near, y_near, out1, in1 = x(near), y(near), line(beyond, OUTWARD), line(near, MIDDLE)
    meta = doubled(meta, x(meta))

    x_near, y_near, out1, in1, y_own, meta, both = together(x_near, y_near, out1, in1, y_own, meta, both)
    third = jnp.where(mid, beyond, out1)
    xy_own, y_third, out2 = x(y_own), y(third), line(in1, OUTWARD)
    meta = doubled(meta, line(meta, ENDS))
    both_other = core(both)

    xy_own, y_third, out2, meta, both_other = together(xy_own, y_third, out2, meta, both_other)
    last = jnp.where(mid, in1, out2)
    x_last, y_last, xy_near, xy_beyond = x(last), y(last), line(xy_own, ENDS), line(xy_own, MIDDLE)
    meta = doubled(meta, line(meta, [(i, i ^ 2) for i in range(narrow)]))

    x_last, y_last, xy_near, xy_beyond, third, meta = together(x_last, y_last, xy_near, xy_beyond, third, meta)
    x_third, xy_last, out3 = x(third), y(x_last), line(xy_beyond, OUTWARD)
    rows = tokens.shape[0]
    mine, others = (0, rows), (rows, rows)
    fed, accs = run(pos, meta, [tokens, cotangent, both_other], [
        (0, "own", [own], [y_own]), (0, "near", [near], [y_near]), (1, "own", [x_own], [xy_own]),
    ], [mine, others], None, False)
    fed, accs = run(pos, meta, fed, [
        (0, "third", [third], [y_third]), (1, "near", [x_near], [xy_near]), (0, "last", [last], [y_last]),
    ], [mine, others], accs, False)

    ending = [(1, "last", [x_last], [xy_last]), (1, "third", [x_third], [xy_beyond, out3])]
    _, sent = run(pos, meta, fed, ending, [others], [accs[1], accs[3]], True)
    got = [core(part) for part in sent]
    _, kept = run(pos, meta, fed, ending, [mine], [accs[0], accs[2]], False)
    return tuple(
        (total + other.astype(jnp.float32)).astype(jnp.bfloat16) for total, other in zip(kept, got)
    )


def solution(mesh):
    rows = P(BOTH, None)
    return jax.shard_map(
        body,
        mesh=mesh,
        in_specs=(rows, rows, P(BOTH, None, None, None), rows, P(BOTH)),
        out_specs=(rows, rows),
        check_vma=False,
    )
```

```python
import functools

import jax
import jax.numpy as jnp
from jax import lax
from jax.experimental import pallas as pl
from jax.experimental.pallas import tpu as pltpu
from jax.sharding import PartitionSpec as P

ROOT_2_OVER_PI = 0.7978845608028654
CUBIC = 0.044715
BOTH = ("wide", "narrow")
LABEL_ROWS = 16
MOST_BLOCKS, MOST_SLOTS = 16, 6
VMEM_LIMIT = 32 * 1024 * 1024
PAIRS_VMEM_LIMIT = 16 * 1024 * 1024

ENDS = [(0, 1), (1, 0), (2, 3), (3, 2)]
MIDDLE = [(1, 2), (2, 1)]
OUTWARD = [(1, 0), (2, 3)]


def gelu_and_slope(v):
    inner = ROOT_2_OVER_PI * (v + CUBIC * (v * v * v))
    t = jnp.tanh(inner)
    cdf = 0.5 * (1.0 + t)
    slope = cdf + (0.5 * v) * (1.0 - t * t) * (ROOT_2_OVER_PI * (1.0 + (3.0 * CUBIC) * (v * v)))
    return v * cdf, slope


def dot_plain(a, b):
    return lax.dot_general(a, b, (((1,), (0,)), ((), ())), preferred_element_type=jnp.float32)


def dot_turned(a, b):
    return lax.dot_general(a, b, (((1,), (1,)), ((), ())), preferred_element_type=jnp.float32)


def lanes(index, width):
    return pl.ds(pl.multiple_of(index * width, width), width)


def run_panel(first, second, width, toks, cots, w1, w2, out_accs, grad_accs):
    (index1, count1), (index2, count2) = first, second
    slots = len(index1)

    def kept(parts, index, count, j):
        at = lanes(index[j], width)
        value = jnp.concatenate([part[:, at] for part in parts], axis=0)
        return value if j == 0 else jnp.where(j < count, value, jnp.zeros_like(value))

    pre = dot_plain(kept(toks, index1, count1, 0), w1(0))
    gact = dot_turned(kept(cots, index2, count2, 0), w2(0))
    for j in range(1, slots):
        pre = pre + dot_plain(kept(toks, index1, count1, j), w1(j))
    for j in range(1, slots):
        gact = gact + dot_turned(kept(cots, index2, count2, j), w2(j))
    act, slope = gelu_and_slope(pre)
    act = act.astype(jnp.bfloat16)
    gpre = (gact * slope).astype(jnp.bfloat16)
    zero = jnp.zeros_like(act)

    def add(accs, block, value):
        at = 0
        for acc in accs:
            rows = acc.shape[0]
            acc[:, lanes(block, width)] += value[at : at + rows]
            at += rows

    for j in range(slots):
        add(out_accs, index2[j], dot_plain(jnp.where(j < count2, act, zero), w2(j)))
    for j in range(slots):
        add(grad_accs, index1[j], dot_turned(jnp.where(j < count1, gpre, zero), w1(j)))


def with_labels(weights, block_index, block_counts):
    _, slots, width, _ = weights.shape
    labels = jnp.concatenate([block_index, block_counts[:, None]], axis=1).astype(weights.dtype)
    labels = jnp.pad(labels, ((0, LABEL_ROWS - 1), (0, width - labels.shape[1])))
    return jnp.concatenate([weights.reshape(slots * width, width), labels], axis=0)


def read_labels(labels, slots):
    values = labels.astype(jnp.float32)
    row = lax.broadcasted_iota(jnp.int32, values.shape, 0)
    lane = lax.broadcasted_iota(jnp.int32, values.shape, 1)
    scale = jnp.zeros_like(values)
    for j in range(slots):
        scale = jnp.where((row == 0) & (lane == j), float(MOST_BLOCKS**j), scale)
    packed = jnp.sum(values * scale).astype(jnp.int32)
    count = jnp.sum(jnp.where((row == 0) & (lane == slots), values, 0.0)).astype(jnp.int32)
    index = [lax.shift_right_logical(packed, 4 * j) & (MOST_BLOCKS - 1) for j in range(slots)]
    return index, count


def pairs_kernel(plan, *refs):
    pairs, spans, starts, rounds, slots, width = (
        plan["pairs"], plan["spans"], plan["starts"], plan["rounds"], plan["slots"], plan["width"],
    )
    n, parts = len(pairs), len(spans)
    refs = list(refs)

    def take(count):
        taken = refs[:count]
        del refs[:count]
        return taken

    (pos,) = take(1)
    fed = take(3 if starts else 2)
    held = [[take(k) for k in counts] for counts in pairs]
    if starts:
        tok, cot = take(2)
    else:
        tok, cot = fed
        take(2 * parts)
    sums = take(2 * parts)
    rounded = take(2 * parts if rounds else 0)
    low, z = pos[0], pos[1]
    middle = (z == 1) | (z == 2)
    if plan["direct"]:
        toks = [tok.at[pl.ds(at, size)] for at, size in spans]
        cots = [cot.at[pl.ds(at, size)] for at, size in spans]
        below = pl.ds(slots * width, LABEL_ROWS)

        def reader(choice):
            if len(choice) == 1:
                return lambda at: choice[0][at, :]
            return lambda at: jnp.where(middle, choice[0][at, :], choice[1][at, :])

        def panels(first):
            for both in held:
                read1, read2 = reader(both[first]), reader(both[1 - first])
                run_panel(
                    read_labels(read1(below), slots), read_labels(read2(below), slots), width, toks, cots,
                    lambda j, read1=read1: read1(pl.ds(j * width, width)),
                    lambda j, read2=read2: read2(pl.ds(j * width, width)),
                    sums[:parts], sums[parts:],
                )

        pl.when(low == 1)(lambda: panels(0))
        pl.when(low == 0)(lambda: panels(1))
        for total, out in zip(sums, rounded):
            out[...] = total[...].astype(out.dtype)
        return
    blocks, block_sem = take(2)

    feeding = []
    if starts:
        own_tok, own_cot, other = fed
        rows = own_tok.shape[0]
        first, second = pl.ds(0, rows), pl.ds(rows, rows)
        feeding = [
            pltpu.make_async_copy(src, dst, refs[0].at[k])
            for k, (src, dst) in enumerate((
                (own_tok, tok.at[first]), (other.at[first], tok.at[second]),
                (own_cot, cot.at[first]), (other.at[second], cot.at[second]),
            ))
        ]
    for copy in feeding:
        copy.start()

    def block_copy(k, side, source):
        return pltpu.make_async_copy(source, blocks.at[k, side], block_sem.at[k, side])

    def begin(k, side):
        for which in range(2):
            choice = held[k][which]
            here = low == (1 if which == side else 0)
            for pick, source in enumerate(choice):
                wanted = here
                if len(choice) == 2:
                    wanted = here & (middle if pick == 0 else jnp.logical_not(middle))
                pl.when(wanted)(lambda source=source: block_copy(k, side, source).start())

    for k in range(n):
        begin(k, 0)
        begin(k, 1)
    if starts:
        for total in sums:
            total[...] = jnp.zeros_like(total)
    for copy in feeding:
        copy.wait()
    toks = [tok.at[pl.ds(at, size)] for at, size in spans]
    cots = [cot.at[pl.ds(at, size)] for at, size in spans]
    for k in range(n):
        rows = []
        for side in range(2):
            block_copy(k, side, held[k][side][0]).wait()
            rows.append(read_labels(blocks[k, side, pl.ds(slots * width, LABEL_ROWS), :], slots))
        run_panel(
            rows[0], rows[1], width, toks, cots,
            lambda j, k=k: blocks[k, 0, pl.ds(j * width, width), :],
            lambda j, k=k: blocks[k, 1, pl.ds(j * width, width), :],
            sums[:parts], sums[parts:],
        )
    for total, out in zip(sums, rounded):
        out[...] = total[...].astype(out.dtype)


def run_pairs(pos, fed, items, spans, accs, rounds, sizes, direct=False):
    slots, width = sizes
    parts, n = len(spans), len(items)
    starts = accs is None
    model = fed[0].shape[1]
    plan = dict(
        pairs=[(len(first), len(second)) for first, second in items],
        spans=spans, starts=starts, rounds=rounds, slots=slots, width=width, direct=direct,
    )
    smem = pl.BlockSpec(memory_space=pltpu.SMEM)
    vmem = pl.BlockSpec(memory_space=pltpu.VMEM)
    hbm = pl.BlockSpec(memory_space=pl.ANY)

    def off_chip(value):
        return pltpu.with_memory_space_constraint(value, pltpu.HBM)

    blocks = [a if direct else off_chip(a) for item in items for choice in item for a in choice]
    if starts:
        fed = [off_chip(value) for value in fed]
    operands = [pos, *fed, *blocks, *(accs or [])]
    first_acc = len(operands) - 2 * parts
    out_shape = [jax.ShapeDtypeStruct((size, model), jnp.float32) for _, size in spans] * 2
    if rounds:
        out_shape += [jax.ShapeDtypeStruct((size, model), jnp.bfloat16) for _, size in spans] * 2
    rows = sum(size for _, size in spans)
    scratch = [pltpu.VMEM((n, 2, slots * width + LABEL_ROWS, width), jnp.bfloat16), pltpu.SemaphoreType.DMA((n, 2))]
    if direct:
        scratch = []
    if starts:
        out_shape = [jax.ShapeDtypeStruct((rows, model), jnp.bfloat16)] * 2 + out_shape
        scratch += [pltpu.SemaphoreType.DMA((4,))]
    outs = pl.pallas_call(
        functools.partial(pairs_kernel, plan),
        out_shape=out_shape,
        in_specs=[smem] + [hbm if starts else vmem] * len(fed) + [vmem if direct else hbm] * len(blocks) + [vmem] * len(accs or []),
        out_specs=[vmem] * len(out_shape),
        scratch_shapes=scratch,
        input_output_aliases={} if starts else {first_acc + i: i for i in range(2 * parts)},
        compiler_params=pltpu.CompilerParams(vmem_limit_bytes=PAIRS_VMEM_LIMIT),
        cost_estimate=pl.CostEstimate(
            flops=n * 4 * slots * 2 * rows * width * width,
            transcendentals=n * rows * width,
            bytes_accessed=2 * n * slots * width * width * 2,
        ),
    )(*operands)
    return (outs[:2] if starts else fed), outs[-2 * parts :]


def all_panels_kernel(slots, width, half, meta, tok, cot, held, out, grad, blocks, out_acc, grad_acc, sem):
    def copies(p, buf):
        return [
            pltpu.make_async_copy(held.at[p], blocks.at[buf, 0], sem.at[buf, 0]),
            pltpu.make_async_copy(held.at[half + p], blocks.at[buf, 1], sem.at[buf, 1]),
        ]

    def row_of(r):
        return [meta[r, j] for j in range(slots)], meta[r, slots]

    out_acc[...] = jnp.zeros_like(out_acc)
    grad_acc[...] = jnp.zeros_like(grad_acc)
    for copy in copies(0, 0):
        copy.start()

    def step(p, _):
        buf = lax.rem(p, 2)

        @pl.when(p + 1 < half)
        def _():
            for copy in copies(p + 1, 1 - buf):
                copy.start()

        for copy in copies(p, buf):
            copy.wait()
        run_panel(
            row_of(p), row_of(half + p), width, [tok], [cot],
            lambda j: blocks[buf, 0, j], lambda j: blocks[buf, 1, j], [out_acc], [grad_acc],
        )
        return 0

    lax.fori_loop(0, half, step, 0)
    out[...] = out_acc[...].astype(out.dtype)
    grad[...] = grad_acc[...].astype(grad.dtype)


def run_all(meta, tokens, cotangent, gathered):
    count, slots, width, _ = gathered.shape
    rows, model = tokens.shape
    vmem = pl.BlockSpec(memory_space=pltpu.VMEM)
    return pl.pallas_call(
        functools.partial(all_panels_kernel, slots, width, count // 2),
        out_shape=[jax.ShapeDtypeStruct((rows, model), jnp.bfloat16)] * 2,
        in_specs=[pl.BlockSpec(memory_space=pltpu.SMEM), vmem, vmem, pl.BlockSpec(memory_space=pl.ANY)],
        out_specs=[vmem] * 2,
        scratch_shapes=[
            pltpu.VMEM((2, 2, slots, width, width), jnp.bfloat16),
            pltpu.VMEM((rows, model), jnp.float32),
            pltpu.VMEM((rows, model), jnp.float32),
            pltpu.SemaphoreType.DMA((2, 2)),
        ],
        compiler_params=pltpu.CompilerParams(vmem_limit_bytes=VMEM_LIMIT),
    )(meta, tokens, cotangent, gathered)


def together(*values):
    return lax.optimization_barrier(values)


def after(value, *others):
    return together(value, *others)[0]


def exchange_plan(wide, narrow, slots, blocks):
    return wide == 8 and narrow == 4 and slots <= MOST_SLOTS and blocks <= MOST_BLOCKS


def body(tokens, cotangent, weights, block_index, block_counts):
    wide, narrow = lax.axis_size("wide"), lax.axis_size("narrow")
    slots, width = weights.shape[1], weights.shape[2]
    if not exchange_plan(wide, narrow, slots, tokens.shape[1] // width):
        own_meta = jnp.concatenate([block_index, block_counts[:, None]], axis=1)
        meta = lax.all_gather(own_meta, BOTH, axis=0, tiled=True)
        gathered = lax.all_gather(weights, BOTH, axis=0, tiled=True)
        return tuple(run_all(meta, tokens, cotangent, gathered))

    def across(value, bit):
        return lax.ppermute(value, "wide", [(i, i ^ bit) for i in range(wide)])

    core, x, y = (functools.partial(across, bit=bit) for bit in (1, 2, 4))

    def line(value, pairs):
        return lax.ppermute(value, "narrow", pairs)

    w, z = lax.axis_index("wide"), lax.axis_index("narrow")
    pos = jnp.stack([(w < wide // 2).astype(jnp.int32), z.astype(jnp.int32)])
    mid = (z == 1) | (z == 2)
    run = functools.partial(run_pairs, sizes=(slots, width))
    rows = tokens.shape[0]
    mine, others = (0, rows), (rows, rows)

    own = with_labels(weights, block_index, block_counts)
    x_own, y_own, near, beyond = x(own), y(own), line(own, ENDS), line(own, MIDDLE)
    x_own, y_own, near, beyond = together(x_own, y_own, near, beyond)
    both = jnp.concatenate([tokens, cotangent], axis=0)

    out1, in1 = line(beyond, OUTWARD), line(near, MIDDLE)
    y_near, xy_own = y(after(near, y_own)), x(after(y_own, x_own))
    both_other = core(after(both, x_own))

    out2, xy_beyond = line(after(in1, out1), OUTWARD), line(after(xy_own, in1), MIDDLE)
    third = jnp.where(mid, beyond, out1)
    y_third, x_near = y(after(third, y_near)), x(after(near, xy_own))

    last = jnp.where(mid, in1, out2)
    x_last, xy_near, y_last = x(after(last, x_near)), line(after(xy_own, out2), ENDS), y(after(last, y_third))
    fed, accs = run(pos, [tokens, cotangent, both_other], [
        ([own], [y_own]), ([near], [y_near]), ([x_own], [xy_own]),
    ], [mine, others], None, False)

    x_third, out3, xy_last = x(after(third, x_last)), line(after(xy_beyond, xy_near), OUTWARD), y(after(x_last, y_last))
    fed, accs = run(pos, fed, [
        ([third], [y_third]), ([x_near], [xy_near]), ([last], [y_last]),
    ], [mine, others], accs, False)

    ending = [([x_last], [xy_last]), ([x_third], [xy_beyond, out3])]
    _, sent = run(pos, fed, ending, [others], [accs[1], accs[3]], True, direct=True)
    got = [core(part) for part in sent]
    _, kept = run(pos, fed, ending, [mine], [accs[0], accs[2]], False, direct=True)
    return tuple(
        (total + other.astype(jnp.float32)).astype(jnp.bfloat16) for total, other in zip(kept, got)
    )


def solution(mesh):
    rows = P(BOTH, None)
    return jax.shard_map(
        body,
        mesh=mesh,
        in_specs=(rows, rows, P(BOTH, None, None, None), rows, P(BOTH)),
        out_specs=(rows, rows),
        check_vma=False,
    )
```

```python
import functools

import jax
import jax.numpy as jnp
from jax import lax
from jax.experimental import pallas as pl
from jax.experimental.pallas import tpu as pltpu
from jax.sharding import PartitionSpec as P

ROOT_2_OVER_PI = 0.7978845608028654
CUBIC = 0.044715
BOTH = ("wide", "narrow")
LABEL_ROWS = 16
MOST_BLOCKS, MOST_SLOTS = 16, 6
VMEM_LIMIT = 32 * 1024 * 1024
PAIRS_VMEM_LIMIT = 16 * 1024 * 1024

ENDS = [(0, 1), (1, 0), (2, 3), (3, 2)]
MIDDLE = [(1, 2), (2, 1)]
OUTWARD = [(1, 0), (2, 3)]


def gelu_and_slope(v):
    inner = ROOT_2_OVER_PI * (v + CUBIC * (v * v * v))
    t = jnp.tanh(inner)
    cdf = 0.5 * (1.0 + t)
    slope = cdf + (0.5 * v) * (1.0 - t * t) * (ROOT_2_OVER_PI * (1.0 + (3.0 * CUBIC) * (v * v)))
    return v * cdf, slope


def dot_plain(a, b):
    return lax.dot_general(a, b, (((1,), (0,)), ((), ())), preferred_element_type=jnp.float32)


def dot_turned(a, b):
    return lax.dot_general(a, b, (((1,), (1,)), ((), ())), preferred_element_type=jnp.float32)


def lanes(index, width):
    return pl.ds(pl.multiple_of(index * width, width), width)


def run_panel(first, second, width, toks, cots, w1, w2, out_accs, grad_accs):
    (index1, count1), (index2, count2) = first, second
    slots = len(index1)

    def kept(parts, index, count, j):
        at = lanes(index[j], width)
        value = jnp.concatenate([part[:, at] for part in parts], axis=0)
        return value if j == 0 else jnp.where(j < count, value, jnp.zeros_like(value))

    pre = dot_plain(kept(toks, index1, count1, 0), w1(0))
    gact = dot_turned(kept(cots, index2, count2, 0), w2(0))
    for j in range(1, slots):
        pre = pre + dot_plain(kept(toks, index1, count1, j), w1(j))
    for j in range(1, slots):
        gact = gact + dot_turned(kept(cots, index2, count2, j), w2(j))
    act, slope = gelu_and_slope(pre)
    act = act.astype(jnp.bfloat16)
    gpre = (gact * slope).astype(jnp.bfloat16)
    zero = jnp.zeros_like(act)

    def add(accs, block, value):
        at = 0
        for acc in accs:
            rows = acc.shape[0]
            acc[:, lanes(block, width)] += value[at : at + rows]
            at += rows

    for j in range(slots):
        add(out_accs, index2[j], dot_plain(jnp.where(j < count2, act, zero), w2(j)))
    for j in range(slots):
        add(grad_accs, index1[j], dot_turned(jnp.where(j < count1, gpre, zero), w1(j)))


def with_labels(weights, block_index, block_counts):
    _, slots, width, _ = weights.shape
    labels = jnp.concatenate([block_index, block_counts[:, None]], axis=1).astype(weights.dtype)
    labels = jnp.pad(labels, ((0, LABEL_ROWS - 1), (0, width - labels.shape[1])))
    return jnp.concatenate([weights.reshape(slots * width, width), labels], axis=0)


def read_labels(labels, slots):
    values = labels.astype(jnp.float32)
    row = lax.broadcasted_iota(jnp.int32, values.shape, 0)
    lane = lax.broadcasted_iota(jnp.int32, values.shape, 1)
    scale = jnp.zeros_like(values)
    for j in range(slots):
        scale = jnp.where((row == 0) & (lane == j), float(MOST_BLOCKS**j), scale)
    packed = jnp.sum(values * scale).astype(jnp.int32)
    count = jnp.sum(jnp.where((row == 0) & (lane == slots), values, 0.0)).astype(jnp.int32)
    index = [lax.shift_right_logical(packed, 4 * j) & (MOST_BLOCKS - 1) for j in range(slots)]
    return index, count


def pairs_kernel(plan, *refs):
    pairs, spans, starts, rounds, slots, width = (
        plan["pairs"], plan["spans"], plan["starts"], plan["rounds"], plan["slots"], plan["width"],
    )
    n, parts = len(pairs), len(spans)
    refs = list(refs)

    def take(count):
        taken = refs[:count]
        del refs[:count]
        return taken

    (pos,) = take(1)
    fed = take(3 if starts else 2)
    held = [[take(k) for k in counts] for counts in pairs]
    if starts:
        tok, cot = take(2)
    else:
        tok, cot = fed
        take(2 * parts)
    sums = take(2 * parts)
    rounded = take(2 * parts if rounds else 0)
    low, z = pos[0], pos[1]
    middle = (z == 1) | (z == 2)
    if plan["direct"]:
        toks = [tok.at[pl.ds(at, size)] for at, size in spans]
        cots = [cot.at[pl.ds(at, size)] for at, size in spans]
        below = pl.ds(slots * width, LABEL_ROWS)

        def reader(choice):
            if len(choice) == 1:
                return lambda at: choice[0][at, :]
            return lambda at: jnp.where(middle, choice[0][at, :], choice[1][at, :])

        def panels(first):
            for both in held:
                read1, read2 = reader(both[first]), reader(both[1 - first])
                run_panel(
                    read_labels(read1(below), slots), read_labels(read2(below), slots), width, toks, cots,
                    lambda j, read1=read1: read1(pl.ds(j * width, width)),
                    lambda j, read2=read2: read2(pl.ds(j * width, width)),
                    sums[:parts], sums[parts:],
                )

        pl.when(low == 1)(lambda: panels(0))
        pl.when(low == 0)(lambda: panels(1))
        for total, out in zip(sums, rounded):
            out[...] = total[...].astype(out.dtype)
        return
    blocks, block_sem = take(2)

    feeding = []
    if starts:
        own_tok, own_cot, other = fed
        rows = own_tok.shape[0]
        first, second = pl.ds(0, rows), pl.ds(rows, rows)
        feeding = [
            pltpu.make_async_copy(src, dst, refs[0].at[k])
            for k, (src, dst) in enumerate((
                (own_tok, tok.at[first]), (other.at[first], tok.at[second]),
                (own_cot, cot.at[first]), (other.at[second], cot.at[second]),
            ))
        ]
    for copy in feeding:
        copy.start()

    def block_copy(k, side, source):
        return pltpu.make_async_copy(source, blocks.at[k, side], block_sem.at[k, side])

    def begin(k, side):
        for which in range(2):
            choice = held[k][which]
            here = low == (1 if which == side else 0)
            for pick, source in enumerate(choice):
                wanted = here
                if len(choice) == 2:
                    wanted = here & (middle if pick == 0 else jnp.logical_not(middle))
                pl.when(wanted)(lambda source=source: block_copy(k, side, source).start())

    for k in range(n):
        begin(k, 0)
        begin(k, 1)
    if starts:
        for total in sums:
            total[...] = jnp.zeros_like(total)
    for copy in feeding:
        copy.wait()
    toks = [tok.at[pl.ds(at, size)] for at, size in spans]
    cots = [cot.at[pl.ds(at, size)] for at, size in spans]
    for k in range(n):
        rows = []
        for side in range(2):
            block_copy(k, side, held[k][side][0]).wait()
            rows.append(read_labels(blocks[k, side, pl.ds(slots * width, LABEL_ROWS), :], slots))
        run_panel(
            rows[0], rows[1], width, toks, cots,
            lambda j, k=k: blocks[k, 0, pl.ds(j * width, width), :],
            lambda j, k=k: blocks[k, 1, pl.ds(j * width, width), :],
            sums[:parts], sums[parts:],
        )
    for total, out in zip(sums, rounded):
        out[...] = total[...].astype(out.dtype)


def run_pairs(pos, fed, items, spans, accs, rounds, sizes, direct=False):
    slots, width = sizes
    parts, n = len(spans), len(items)
    starts = accs is None
    model = fed[0].shape[1]
    plan = dict(
        pairs=[(len(first), len(second)) for first, second in items],
        spans=spans, starts=starts, rounds=rounds, slots=slots, width=width, direct=direct,
    )
    smem = pl.BlockSpec(memory_space=pltpu.SMEM)
    vmem = pl.BlockSpec(memory_space=pltpu.VMEM)
    hbm = pl.BlockSpec(memory_space=pl.ANY)

    def off_chip(value):
        return pltpu.with_memory_space_constraint(value, pltpu.HBM)

    blocks = [a if direct else off_chip(a) for item in items for choice in item for a in choice]
    if starts:
        fed = [off_chip(value) for value in fed]
    operands = [pos, *fed, *blocks, *(accs or [])]
    first_acc = len(operands) - 2 * parts
    out_shape = [jax.ShapeDtypeStruct((size, model), jnp.float32) for _, size in spans] * 2
    if rounds:
        out_shape += [jax.ShapeDtypeStruct((size, model), jnp.bfloat16) for _, size in spans] * 2
    rows = sum(size for _, size in spans)
    scratch = [pltpu.VMEM((n, 2, slots * width + LABEL_ROWS, width), jnp.bfloat16), pltpu.SemaphoreType.DMA((n, 2))]
    if direct:
        scratch = []
    if starts:
        out_shape = [jax.ShapeDtypeStruct((rows, model), jnp.bfloat16)] * 2 + out_shape
        scratch += [pltpu.SemaphoreType.DMA((4,))]
    outs = pl.pallas_call(
        functools.partial(pairs_kernel, plan),
        out_shape=out_shape,
        in_specs=[smem] + [hbm if starts else vmem] * len(fed) + [vmem if direct else hbm] * len(blocks) + [vmem] * len(accs or []),
        out_specs=[vmem] * len(out_shape),
        scratch_shapes=scratch,
        input_output_aliases={} if starts else {first_acc + i: i for i in range(2 * parts)},
        compiler_params=pltpu.CompilerParams(vmem_limit_bytes=PAIRS_VMEM_LIMIT),
        cost_estimate=pl.CostEstimate(
            flops=n * 4 * slots * 2 * rows * width * width,
            transcendentals=n * rows * width,
            bytes_accessed=2 * n * slots * width * width * 2,
        ),
    )(*operands)
    return (outs[:2] if starts else fed), outs[-2 * parts :]


def all_panels_kernel(slots, width, half, meta, tok, cot, held, out, grad, blocks, out_acc, grad_acc, sem):
    def copies(p, buf):
        return [
            pltpu.make_async_copy(held.at[p], blocks.at[buf, 0], sem.at[buf, 0]),
            pltpu.make_async_copy(held.at[half + p], blocks.at[buf, 1], sem.at[buf, 1]),
        ]

    def row_of(r):
        return [meta[r, j] for j in range(slots)], meta[r, slots]

    out_acc[...] = jnp.zeros_like(out_acc)
    grad_acc[...] = jnp.zeros_like(grad_acc)
    for copy in copies(0, 0):
        copy.start()

    def step(p, _):
        buf = lax.rem(p, 2)

        @pl.when(p + 1 < half)
        def _():
            for copy in copies(p + 1, 1 - buf):
                copy.start()

        for copy in copies(p, buf):
            copy.wait()
        run_panel(
            row_of(p), row_of(half + p), width, [tok], [cot],
            lambda j: blocks[buf, 0, j], lambda j: blocks[buf, 1, j], [out_acc], [grad_acc],
        )
        return 0

    lax.fori_loop(0, half, step, 0)
    out[...] = out_acc[...].astype(out.dtype)
    grad[...] = grad_acc[...].astype(grad.dtype)


def run_all(meta, tokens, cotangent, gathered):
    count, slots, width, _ = gathered.shape
    rows, model = tokens.shape
    vmem = pl.BlockSpec(memory_space=pltpu.VMEM)
    return pl.pallas_call(
        functools.partial(all_panels_kernel, slots, width, count // 2),
        out_shape=[jax.ShapeDtypeStruct((rows, model), jnp.bfloat16)] * 2,
        in_specs=[pl.BlockSpec(memory_space=pltpu.SMEM), vmem, vmem, pl.BlockSpec(memory_space=pl.ANY)],
        out_specs=[vmem] * 2,
        scratch_shapes=[
            pltpu.VMEM((2, 2, slots, width, width), jnp.bfloat16),
            pltpu.VMEM((rows, model), jnp.float32),
            pltpu.VMEM((rows, model), jnp.float32),
            pltpu.SemaphoreType.DMA((2, 2)),
        ],
        compiler_params=pltpu.CompilerParams(vmem_limit_bytes=VMEM_LIMIT),
    )(meta, tokens, cotangent, gathered)


def together(*values):
    return lax.optimization_barrier(values)


def after(value, *others):
    return together(value, *others)[0]


def exchange_plan(wide, narrow, slots, blocks):
    return wide == 8 and narrow == 4 and slots <= MOST_SLOTS and blocks <= MOST_BLOCKS


def body(tokens, cotangent, weights, block_index, block_counts):
    wide, narrow = lax.axis_size("wide"), lax.axis_size("narrow")
    slots, width = weights.shape[1], weights.shape[2]
    if not exchange_plan(wide, narrow, slots, tokens.shape[1] // width):
        own_meta = jnp.concatenate([block_index, block_counts[:, None]], axis=1)
        meta = lax.all_gather(own_meta, BOTH, axis=0, tiled=True)
        gathered = lax.all_gather(weights, BOTH, axis=0, tiled=True)
        return tuple(run_all(meta, tokens, cotangent, gathered))

    def across(value, bit):
        return lax.ppermute(value, "wide", [(i, i ^ bit) for i in range(wide)])

    core, x, y = (functools.partial(across, bit=bit) for bit in (1, 2, 4))

    def line(value, pairs):
        return lax.ppermute(value, "narrow", pairs)

    w, z = lax.axis_index("wide"), lax.axis_index("narrow")
    pos = jnp.stack([(w < wide // 2).astype(jnp.int32), z.astype(jnp.int32)])
    mid = (z == 1) | (z == 2)
    run = functools.partial(run_pairs, sizes=(slots, width))
    rows = tokens.shape[0]
    mine, others = (0, rows), (rows, rows)

    own = with_labels(weights, block_index, block_counts)
    x_own, y_own, near, beyond = x(own), y(own), line(own, ENDS), line(own, MIDDLE)
    x_own, y_own, near, beyond = together(x_own, y_own, near, beyond)
    both = jnp.concatenate([tokens, cotangent], axis=0)

    out1, in1 = line(beyond, OUTWARD), line(near, MIDDLE)
    y_near, xy_own = y(after(near, y_own)), x(after(y_own, x_own))
    both_other = core(after(both, x_own))

    out2, xy_beyond = line(after(in1, out1), OUTWARD), line(after(xy_own, in1), MIDDLE)
    third = jnp.where(mid, beyond, out1)
    y_third, x_near = y(after(third, y_near)), x(after(near, xy_own))

    last = jnp.where(mid, in1, out2)
    x_last, xy_near, y_last = x(after(last, x_near)), line(after(xy_own, out2), ENDS), y(after(last, y_third))
    fed, accs = run(pos, [tokens, cotangent, both_other], [
        ([own], [y_own]), ([near], [y_near]), ([x_own], [xy_own]),
    ], [mine, others], None, False)

    xy_last, x_third, out3 = y(after(x_last, y_last)), x(after(third, x_last)), line(after(xy_beyond, xy_near), OUTWARD)
    fed, accs = run(pos, fed, [
        ([beyond, out1], [y_third]), ([x_near], [xy_near]), ([in1, out2], [y_last]),
    ], [mine, others], accs, False)

    ending = [([x_last], [xy_last]), ([x_third], [xy_beyond, out3])]
    _, sent = run(pos, fed, ending, [others], [accs[1], accs[3]], True, direct=True)
    got = [core(part) for part in sent]
    _, kept = run(pos, fed, ending, [mine], [accs[0], accs[2]], False, direct=True)
    return tuple(
        (total + other.astype(jnp.float32)).astype(jnp.bfloat16) for total, other in zip(kept, got)
    )


def solution(mesh):
    rows = P(BOTH, None)
    return jax.shard_map(
        body,
        mesh=mesh,
        in_specs=(rows, rows, P(BOTH, None, None, None), rows, P(BOTH)),
        out_specs=(rows, rows),
        check_vma=False,
    )
```

```python
import functools

import jax
import jax.numpy as jnp
from jax import lax
from jax.experimental import pallas as pl
from jax.experimental.pallas import tpu as pltpu
from jax.sharding import PartitionSpec as P

ROOT_2_OVER_PI = 0.7978845608028654
CUBIC = 0.044715
BOTH = ("wide", "narrow")
LABEL_ROWS = 16
ADD_STEPS = 4
MOST_BLOCKS, MOST_SLOTS = 16, 6
VMEM_LIMIT = 32 * 1024 * 1024
PAIRS_VMEM_LIMIT = 16 * 1024 * 1024

ENDS = [(0, 1), (1, 0), (2, 3), (3, 2)]
MIDDLE = [(1, 2), (2, 1)]
OUTWARD = [(1, 0), (2, 3)]


def gelu_and_slope(v):
    inner = ROOT_2_OVER_PI * (v + CUBIC * (v * v * v))
    t = jnp.tanh(inner)
    cdf = 0.5 * (1.0 + t)
    slope = cdf + (0.5 * v) * (1.0 - t * t) * (ROOT_2_OVER_PI * (1.0 + (3.0 * CUBIC) * (v * v)))
    return v * cdf, slope


def dot_plain(a, b):
    return lax.dot_general(a, b, (((1,), (0,)), ((), ())), preferred_element_type=jnp.float32)


def dot_turned(a, b):
    return lax.dot_general(a, b, (((1,), (1,)), ((), ())), preferred_element_type=jnp.float32)


def lanes(index, width):
    return pl.ds(pl.multiple_of(index * width, width), width)


def run_panel(first, second, width, toks, cots, w1, w2, out_accs, grad_accs):
    (index1, count1), (index2, count2) = first, second
    slots = len(index1)

    def kept(parts, index, count, j):
        at = lanes(index[j], width)
        value = jnp.concatenate([part[:, at] for part in parts], axis=0)
        return value if j == 0 else jnp.where(j < count, value, jnp.zeros_like(value))

    pre = dot_plain(kept(toks, index1, count1, 0), w1(0))
    gact = dot_turned(kept(cots, index2, count2, 0), w2(0))
    for j in range(1, slots):
        pre = pre + dot_plain(kept(toks, index1, count1, j), w1(j))
    for j in range(1, slots):
        gact = gact + dot_turned(kept(cots, index2, count2, j), w2(j))
    act, slope = gelu_and_slope(pre)
    act = act.astype(jnp.bfloat16)
    gpre = (gact * slope).astype(jnp.bfloat16)
    zero = jnp.zeros_like(act)

    def add(accs, block, value):
        at = 0
        for acc in accs:
            rows = acc.shape[0]
            acc[:, lanes(block, width)] += value[at : at + rows]
            at += rows

    for j in range(slots):
        add(out_accs, index2[j], dot_plain(jnp.where(j < count2, act, zero), w2(j)))
    for j in range(slots):
        add(grad_accs, index1[j], dot_turned(jnp.where(j < count1, gpre, zero), w1(j)))


def with_labels(weights, block_index, block_counts):
    _, slots, width, _ = weights.shape
    row = lax.broadcasted_iota(jnp.int32, (LABEL_ROWS, width), 0)
    lane = lax.broadcasted_iota(jnp.int32, (LABEL_ROWS, width), 1)
    count = jnp.where((row == 0) & (lane == slots), lax.reshape(block_counts, ()), 0)
    labels = jnp.pad(block_index, ((0, LABEL_ROWS - 1), (0, width - slots))) + count
    labels = labels.astype(weights.dtype)
    return jnp.concatenate([weights.reshape(slots * width, width), labels], axis=0)


def add_kernel(*refs):
    n = (len(refs) - 2) // 3
    totals, others, outs = refs[:n], refs[n : 2 * n], refs[2 * n : 3 * n]
    staged, sem = refs[3 * n :]
    step = totals[0].shape[0] // ADD_STEPS
    copies = []
    for k in range(n):
        for i in range(ADD_STEPS):
            at = pl.ds(i * step, step)
            staged[k, at, :] = (totals[k][at, :] + others[k][at, :].astype(jnp.float32)).astype(staged.dtype)
            copies.append(pltpu.make_async_copy(staged.at[k, at], outs[k].at[at], sem.at[k, i]))
            copies[-1].start()
    for copy in copies:
        copy.wait()


def add_rounded(totals, others):
    n = len(totals)
    vmem, hbm = pl.BlockSpec(memory_space=pltpu.VMEM), pl.BlockSpec(memory_space=pl.ANY)
    shape = jax.ShapeDtypeStruct(totals[0].shape, jnp.bfloat16)
    return pl.pallas_call(
        add_kernel,
        out_shape=[shape] * n,
        in_specs=[vmem] * (2 * n),
        out_specs=[hbm] * n,
        scratch_shapes=[pltpu.VMEM((n,) + shape.shape, shape.dtype), pltpu.SemaphoreType.DMA((n, ADD_STEPS))],
        compiler_params=pltpu.CompilerParams(vmem_limit_bytes=PAIRS_VMEM_LIMIT),
    )(*totals, *others)


def read_labels(labels, slots):
    values = labels.astype(jnp.float32)
    row = lax.broadcasted_iota(jnp.int32, values.shape, 0)
    lane = lax.broadcasted_iota(jnp.int32, values.shape, 1)
    scale = jnp.zeros_like(values)
    for j in range(slots):
        scale = jnp.where((row == 0) & (lane == j), float(MOST_BLOCKS**j), scale)
    packed = jnp.sum(values * scale).astype(jnp.int32)
    count = jnp.sum(jnp.where((row == 0) & (lane == slots), values, 0.0)).astype(jnp.int32)
    index = [lax.shift_right_logical(packed, 4 * j) & (MOST_BLOCKS - 1) for j in range(slots)]
    return index, count


def pairs_kernel(plan, *refs):
    pairs, spans, starts, rounds, slots, width = (
        plan["pairs"], plan["spans"], plan["starts"], plan["rounds"], plan["slots"], plan["width"],
    )
    n, parts = len(pairs), len(spans)
    refs = list(refs)

    def take(count):
        taken = refs[:count]
        del refs[:count]
        return taken

    (pos,) = take(1)
    fed = take(3 if starts else 2)
    held = [[take(k) for k in counts] for counts in pairs]
    if starts:
        tok, cot = take(2)
    else:
        tok, cot = fed
        take(2 * parts)
    sums = take(2 * parts)
    rounded = take(2 * parts if rounds else 0)
    low, z = pos[0], pos[1]
    middle = (z == 1) | (z == 2)
    if plan["direct"]:
        toks = [tok.at[pl.ds(at, size)] for at, size in spans]
        cots = [cot.at[pl.ds(at, size)] for at, size in spans]
        below = pl.ds(slots * width, LABEL_ROWS)

        def reader(choice):
            if len(choice) == 1:
                return lambda at: choice[0][at, :]
            return lambda at: jnp.where(middle, choice[0][at, :], choice[1][at, :])

        def panels(first):
            for both in held:
                read1, read2 = reader(both[first]), reader(both[1 - first])
                run_panel(
                    read_labels(read1(below), slots), read_labels(read2(below), slots), width, toks, cots,
                    lambda j, read1=read1: read1(pl.ds(j * width, width)),
                    lambda j, read2=read2: read2(pl.ds(j * width, width)),
                    sums[:parts], sums[parts:],
                )

        pl.when(low == 1)(lambda: panels(0))
        pl.when(low == 0)(lambda: panels(1))
        for total, out in zip(sums, rounded):
            out[...] = total[...].astype(out.dtype)
        return
    blocks, block_sem = take(2)

    feeding = []
    if starts:
        own_tok, own_cot, other = fed
        rows = own_tok.shape[0]
        first, second = pl.ds(0, rows), pl.ds(rows, rows)
        feeding = [
            pltpu.make_async_copy(src, dst, refs[0].at[k])
            for k, (src, dst) in enumerate((
                (own_tok, tok.at[first]), (other.at[first], tok.at[second]),
                (own_cot, cot.at[first]), (other.at[second], cot.at[second]),
            ))
        ]
    for copy in feeding:
        copy.start()

    def block_copy(k, side, source):
        return pltpu.make_async_copy(source, blocks.at[k, side], block_sem.at[k, side])

    def begin(k, side):
        for which in range(2):
            choice = held[k][which]
            here = low == (1 if which == side else 0)
            for pick, source in enumerate(choice):
                wanted = here
                if len(choice) == 2:
                    wanted = here & (middle if pick == 0 else jnp.logical_not(middle))
                pl.when(wanted)(lambda source=source: block_copy(k, side, source).start())

    for k in range(n):
        begin(k, 0)
        begin(k, 1)
    if starts:
        for total in sums:
            total[...] = jnp.zeros_like(total)
    for copy in feeding:
        copy.wait()
    toks = [tok.at[pl.ds(at, size)] for at, size in spans]
    cots = [cot.at[pl.ds(at, size)] for at, size in spans]
    for k in range(n):
        rows = []
        for side in range(2):
            block_copy(k, side, held[k][side][0]).wait()
            rows.append(read_labels(blocks[k, side, pl.ds(slots * width, LABEL_ROWS), :], slots))
        run_panel(
            rows[0], rows[1], width, toks, cots,
            lambda j, k=k: blocks[k, 0, pl.ds(j * width, width), :],
            lambda j, k=k: blocks[k, 1, pl.ds(j * width, width), :],
            sums[:parts], sums[parts:],
        )
    for total, out in zip(sums, rounded):
        out[...] = total[...].astype(out.dtype)


def run_pairs(pos, fed, items, spans, accs, rounds, sizes, direct=False):
    slots, width = sizes
    parts, n = len(spans), len(items)
    starts = accs is None
    model = fed[0].shape[1]
    plan = dict(
        pairs=[(len(first), len(second)) for first, second in items],
        spans=spans, starts=starts, rounds=rounds, slots=slots, width=width, direct=direct,
    )
    smem = pl.BlockSpec(memory_space=pltpu.SMEM)
    vmem = pl.BlockSpec(memory_space=pltpu.VMEM)
    hbm = pl.BlockSpec(memory_space=pl.ANY)

    def off_chip(value):
        return pltpu.with_memory_space_constraint(value, pltpu.HBM)

    def on_chip(value):
        return pltpu.with_memory_space_constraint(value, pltpu.VMEM)

    blocks = [on_chip(a) if direct else off_chip(a) for item in items for choice in item for a in choice]
    if starts:
        fed = [off_chip(value) for value in fed]
    operands = [pos, *fed, *blocks, *(accs or [])]
    first_acc = len(operands) - 2 * parts
    out_shape = [jax.ShapeDtypeStruct((size, model), jnp.float32) for _, size in spans] * 2
    if rounds:
        out_shape += [jax.ShapeDtypeStruct((size, model), jnp.bfloat16) for _, size in spans] * 2
    rows = sum(size for _, size in spans)
    scratch = [pltpu.VMEM((n, 2, slots * width + LABEL_ROWS, width), jnp.bfloat16), pltpu.SemaphoreType.DMA((n, 2))]
    if direct:
        scratch = []
    if starts:
        out_shape = [jax.ShapeDtypeStruct((rows, model), jnp.bfloat16)] * 2 + out_shape
        scratch += [pltpu.SemaphoreType.DMA((4,))]
    outs = pl.pallas_call(
        functools.partial(pairs_kernel, plan),
        out_shape=out_shape,
        in_specs=[smem] + [hbm if starts else vmem] * len(fed) + [vmem if direct else hbm] * len(blocks) + [vmem] * len(accs or []),
        out_specs=[vmem] * len(out_shape),
        scratch_shapes=scratch,
        input_output_aliases={} if starts else {first_acc + i: i for i in range(2 * parts)},
        compiler_params=pltpu.CompilerParams(vmem_limit_bytes=PAIRS_VMEM_LIMIT),
        cost_estimate=pl.CostEstimate(
            flops=n * 4 * slots * 2 * rows * width * width,
            transcendentals=n * rows * width,
            bytes_accessed=2 * n * slots * width * width * 2,
        ),
    )(*operands)
    return (outs[:2] if starts else fed), outs[-2 * parts :]


def all_panels_kernel(slots, width, half, meta, tok, cot, held, out, grad, blocks, out_acc, grad_acc, sem):
    def copies(p, buf):
        return [
            pltpu.make_async_copy(held.at[p], blocks.at[buf, 0], sem.at[buf, 0]),
            pltpu.make_async_copy(held.at[half + p], blocks.at[buf, 1], sem.at[buf, 1]),
        ]

    def row_of(r):
        return [meta[r, j] for j in range(slots)], meta[r, slots]

    out_acc[...] = jnp.zeros_like(out_acc)
    grad_acc[...] = jnp.zeros_like(grad_acc)
    for copy in copies(0, 0):
        copy.start()

    def step(p, _):
        buf = lax.rem(p, 2)

        @pl.when(p + 1 < half)
        def _():
            for copy in copies(p + 1, 1 - buf):
                copy.start()

        for copy in copies(p, buf):
            copy.wait()
        run_panel(
            row_of(p), row_of(half + p), width, [tok], [cot],
            lambda j: blocks[buf, 0, j], lambda j: blocks[buf, 1, j], [out_acc], [grad_acc],
        )
        return 0

    lax.fori_loop(0, half, step, 0)
    out[...] = out_acc[...].astype(out.dtype)
    grad[...] = grad_acc[...].astype(grad.dtype)


def run_all(meta, tokens, cotangent, gathered):
    count, slots, width, _ = gathered.shape
    rows, model = tokens.shape
    vmem = pl.BlockSpec(memory_space=pltpu.VMEM)
    return pl.pallas_call(
        functools.partial(all_panels_kernel, slots, width, count // 2),
        out_shape=[jax.ShapeDtypeStruct((rows, model), jnp.bfloat16)] * 2,
        in_specs=[pl.BlockSpec(memory_space=pltpu.SMEM), vmem, vmem, pl.BlockSpec(memory_space=pl.ANY)],
        out_specs=[vmem] * 2,
        scratch_shapes=[
            pltpu.VMEM((2, 2, slots, width, width), jnp.bfloat16),
            pltpu.VMEM((rows, model), jnp.float32),
            pltpu.VMEM((rows, model), jnp.float32),
            pltpu.SemaphoreType.DMA((2, 2)),
        ],
        compiler_params=pltpu.CompilerParams(vmem_limit_bytes=VMEM_LIMIT),
    )(meta, tokens, cotangent, gathered)


def together(*values):
    return lax.optimization_barrier(values)


def after(value, *others):
    return together(value, *others)[0]


def exchange_plan(wide, narrow, slots, blocks):
    return wide == 8 and narrow == 4 and slots <= MOST_SLOTS and blocks <= MOST_BLOCKS


def body(tokens, cotangent, weights, block_index, block_counts):
    wide, narrow = lax.axis_size("wide"), lax.axis_size("narrow")
    slots, width = weights.shape[1], weights.shape[2]
    if not exchange_plan(wide, narrow, slots, tokens.shape[1] // width):
        own_meta = jnp.concatenate([block_index, block_counts[:, None]], axis=1)
        meta = lax.all_gather(own_meta, BOTH, axis=0, tiled=True)
        gathered = lax.all_gather(weights, BOTH, axis=0, tiled=True)
        return tuple(run_all(meta, tokens, cotangent, gathered))

    def across(value, bit):
        return lax.ppermute(value, "wide", [(i, i ^ bit) for i in range(wide)])

    core, x, y = (functools.partial(across, bit=bit) for bit in (1, 2, 4))

    def line(value, pairs):
        return lax.ppermute(value, "narrow", pairs)

    w, z = lax.axis_index("wide"), lax.axis_index("narrow")
    pos = jnp.stack([(w < wide // 2).astype(jnp.int32), z.astype(jnp.int32)])
    mid = (z == 1) | (z == 2)
    run = functools.partial(run_pairs, sizes=(slots, width))
    rows = tokens.shape[0]
    mine, others = (0, rows), (rows, rows)

    own = with_labels(weights, block_index, block_counts)
    x_own, y_own, near, beyond = x(own), y(own), line(own, ENDS), line(own, MIDDLE)
    x_own, y_own, near, beyond = together(x_own, y_own, near, beyond)
    both = jnp.concatenate([tokens, cotangent], axis=0)

    out1, in1 = line(beyond, OUTWARD), line(near, MIDDLE)
    y_near, xy_own = y(after(near, y_own)), x(after(y_own, x_own))
    both_other = core(after(both, x_own))

    out2, xy_beyond = line(after(in1, out1), OUTWARD), line(after(xy_own, in1), MIDDLE)
    third = jnp.where(mid, beyond, out1)
    y_third, x_near = y(after(third, y_near)), x(after(near, xy_own))

    last = jnp.where(mid, in1, out2)
    x_last, xy_near, y_last = x(after(last, x_near)), line(after(xy_own, out2), ENDS), y(after(last, y_third))
    fed, accs = run(pos, [tokens, cotangent, both_other], [
        ([own], [y_own]), ([near], [y_near]), ([x_own], [xy_own]),
    ], [mine, others], None, False)

    xy_last, x_third, out3 = y(after(x_last, y_last)), x(after(third, x_last)), line(after(xy_beyond, xy_near), OUTWARD)
    fed, accs = run(pos, fed, [
        ([beyond, out1], [y_third]), ([x_near], [xy_near]), ([in1, out2], [y_last]),
    ], [mine, others], accs, False)

    ending = [([x_last], [xy_last]), ([x_third], [xy_beyond, out3])]
    _, sent = run(pos, fed, ending, [others], [accs[1], accs[3]], True, direct=True)
    got = [core(part) for part in sent]
    _, kept = run(pos, fed, ending, [mine], [accs[0], accs[2]], False, direct=True)
    return tuple(add_rounded(kept, got))


def solution(mesh):
    rows = P(BOTH, None)
    return jax.shard_map(
        body,
        mesh=mesh,
        in_specs=(rows, rows, P(BOTH, None, None, None), rows, P(BOTH)),
        out_specs=(rows, rows),
        check_vma=False,
    )
```

```python
import functools

import jax
import jax.numpy as jnp
from jax import lax
from jax.experimental import pallas as pl
from jax.experimental.pallas import tpu as pltpu
from jax.sharding import PartitionSpec as P

ROOT_2_OVER_PI = 0.7978845608028654
CUBIC = 0.044715
BOTH = ("wide", "narrow")
LABEL_ROWS = 16
ADD_STEPS = 4
MOST_BLOCKS, MOST_SLOTS = 16, 6
VMEM_LIMIT = 32 * 1024 * 1024
PAIRS_VMEM_LIMIT = 16 * 1024 * 1024

ENDS = [(0, 1), (1, 0), (2, 3), (3, 2)]
MIDDLE = [(1, 2), (2, 1)]
OUTWARD = [(1, 0), (2, 3)]


def gelu_and_slope(v):
    inner = ROOT_2_OVER_PI * (v + CUBIC * (v * v * v))
    t = jnp.tanh(inner)
    cdf = 0.5 * (1.0 + t)
    slope = cdf + (0.5 * v) * (1.0 - t * t) * (ROOT_2_OVER_PI * (1.0 + (3.0 * CUBIC) * (v * v)))
    return v * cdf, slope


def dot_plain(a, b):
    return lax.dot_general(a, b, (((1,), (0,)), ((), ())), preferred_element_type=jnp.float32)


def dot_turned(a, b):
    return lax.dot_general(a, b, (((1,), (1,)), ((), ())), preferred_element_type=jnp.float32)


def lanes(index, width):
    return pl.ds(pl.multiple_of(index * width, width), width)


def run_panel(first, second, width, toks, cots, w1, w2, out_accs, grad_accs):
    (index1, count1), (index2, count2) = first, second
    slots = len(index1)

    def kept(parts, index, count, j):
        at = lanes(index[j], width)
        value = jnp.concatenate([part[:, at] for part in parts], axis=0)
        return value if j == 0 else jnp.where(j < count, value, jnp.zeros_like(value))

    pre = dot_plain(kept(toks, index1, count1, 0), w1(0))
    gact = dot_turned(kept(cots, index2, count2, 0), w2(0))
    for j in range(1, slots):
        pre = pre + dot_plain(kept(toks, index1, count1, j), w1(j))
    for j in range(1, slots):
        gact = gact + dot_turned(kept(cots, index2, count2, j), w2(j))
    act, slope = gelu_and_slope(pre)
    act = act.astype(jnp.bfloat16)
    gpre = (gact * slope).astype(jnp.bfloat16)
    zero = jnp.zeros_like(act)

    def add(accs, block, value):
        at = 0
        for acc in accs:
            rows = acc.shape[0]
            acc[:, lanes(block, width)] += value[at : at + rows]
            at += rows

    for j in range(slots):
        add(out_accs, index2[j], dot_plain(jnp.where(j < count2, act, zero), w2(j)))
    for j in range(slots):
        add(grad_accs, index1[j], dot_turned(jnp.where(j < count1, gpre, zero), w1(j)))


def with_labels(weights, block_index, block_counts):
    _, slots, width, _ = weights.shape
    row = lax.broadcasted_iota(jnp.int32, (LABEL_ROWS, width), 0)
    lane = lax.broadcasted_iota(jnp.int32, (LABEL_ROWS, width), 1)
    count = jnp.where((row == 0) & (lane == slots), lax.reshape(block_counts, ()), 0)
    labels = jnp.pad(block_index, ((0, LABEL_ROWS - 1), (0, width - slots))) + count
    labels = labels.astype(weights.dtype)
    return jnp.concatenate([weights.reshape(slots * width, width), labels], axis=0)


def add_kernel(*refs):
    n = (len(refs) - 2) // 3
    totals, others, outs = refs[:n], refs[n : 2 * n], refs[2 * n : 3 * n]
    staged, sem = refs[3 * n :]
    step = totals[0].shape[0] // ADD_STEPS
    copies = []
    for k in range(n):
        for i in range(ADD_STEPS):
            at = pl.ds(i * step, step)
            staged[k, at, :] = (totals[k][at, :] + others[k][at, :].astype(jnp.float32)).astype(staged.dtype)
            copies.append(pltpu.make_async_copy(staged.at[k, at], outs[k].at[at], sem.at[k, i]))
            copies[-1].start()
    for copy in copies:
        copy.wait()


def add_rounded(totals, others):
    n = len(totals)
    vmem, hbm = pl.BlockSpec(memory_space=pltpu.VMEM), pl.BlockSpec(memory_space=pl.ANY)
    shape = jax.ShapeDtypeStruct(totals[0].shape, jnp.bfloat16)
    return pl.pallas_call(
        add_kernel,
        out_shape=[shape] * n,
        in_specs=[vmem] * (2 * n),
        out_specs=[hbm] * n,
        scratch_shapes=[pltpu.VMEM((n,) + shape.shape, shape.dtype), pltpu.SemaphoreType.DMA((n, ADD_STEPS))],
        compiler_params=pltpu.CompilerParams(vmem_limit_bytes=PAIRS_VMEM_LIMIT),
    )(*totals, *others)


def read_labels(labels, slots):
    values = labels.astype(jnp.float32)
    row = lax.broadcasted_iota(jnp.int32, values.shape, 0)
    lane = lax.broadcasted_iota(jnp.int32, values.shape, 1)
    scale = jnp.zeros_like(values)
    for j in range(slots):
        scale = jnp.where((row == 0) & (lane == j), float(MOST_BLOCKS**j), scale)
    packed = jnp.sum(values * scale).astype(jnp.int32)
    count = jnp.sum(jnp.where((row == 0) & (lane == slots), values, 0.0)).astype(jnp.int32)
    index = [lax.shift_right_logical(packed, 4 * j) & (MOST_BLOCKS - 1) for j in range(slots)]
    return index, count


def pairs_kernel(plan, *refs):
    pairs, spans, starts, rounds, slots, width = (
        plan["pairs"], plan["spans"], plan["starts"], plan["rounds"], plan["slots"], plan["width"],
    )
    n, parts = len(pairs), len(spans)
    refs = list(refs)

    def take(count):
        taken = refs[:count]
        del refs[:count]
        return taken

    (pos,) = take(1)
    fed = take(3 if starts else 2)
    held = [[take(k) for k in counts] for counts in pairs]
    if starts:
        tok, cot = take(2)
    else:
        tok, cot = fed
        take(2 * parts)
    sums = take(2 * parts)
    rounded = take(2 * parts if rounds else 0)
    low, z = pos[0], pos[1]
    middle = (z == 1) | (z == 2)
    if plan["direct"]:
        toks = [tok.at[pl.ds(at, size)] for at, size in spans]
        cots = [cot.at[pl.ds(at, size)] for at, size in spans]
        below = pl.ds(slots * width, LABEL_ROWS)

        def reader(choice):
            if len(choice) == 1:
                return lambda at: choice[0][at, :]
            return lambda at: jnp.where(middle, choice[0][at, :], choice[1][at, :])

        def panels(first):
            for both in held:
                read1, read2 = reader(both[first]), reader(both[1 - first])
                run_panel(
                    read_labels(read1(below), slots), read_labels(read2(below), slots), width, toks, cots,
                    lambda j, read1=read1: read1(pl.ds(j * width, width)),
                    lambda j, read2=read2: read2(pl.ds(j * width, width)),
                    sums[:parts], sums[parts:],
                )

        pl.when(low == 1)(lambda: panels(0))
        pl.when(low == 0)(lambda: panels(1))
        for total, out in zip(sums, rounded):
            out[...] = total[...].astype(out.dtype)
        return
    blocks, block_sem = take(2)

    feeding = []
    if starts:
        own_tok, own_cot, other = fed
        rows = own_tok.shape[0]
        first, second = pl.ds(0, rows), pl.ds(rows, rows)
        feeding = [
            pltpu.make_async_copy(src, dst, refs[0].at[k])
            for k, (src, dst) in enumerate((
                (own_tok, tok.at[first]), (other.at[first], tok.at[second]),
                (own_cot, cot.at[first]), (other.at[second], cot.at[second]),
            ))
        ]
    for copy in feeding:
        copy.start()

    def block_copy(k, side, source):
        return pltpu.make_async_copy(source, blocks.at[k, side], block_sem.at[k, side])

    def begin(k, side):
        for which in range(2):
            choice = held[k][which]
            here = low == (1 if which == side else 0)
            for pick, source in enumerate(choice):
                wanted = here
                if len(choice) == 2:
                    wanted = here & (middle if pick == 0 else jnp.logical_not(middle))
                pl.when(wanted)(lambda source=source: block_copy(k, side, source).start())

    for k in range(n):
        begin(k, 0)
        begin(k, 1)
    if starts:
        for total in sums:
            total[...] = jnp.zeros_like(total)
    for copy in feeding:
        copy.wait()
    toks = [tok.at[pl.ds(at, size)] for at, size in spans]
    cots = [cot.at[pl.ds(at, size)] for at, size in spans]
    for k in range(n):
        rows = []
        for side in range(2):
            block_copy(k, side, held[k][side][0]).wait()
            rows.append(read_labels(blocks[k, side, pl.ds(slots * width, LABEL_ROWS), :], slots))
        run_panel(
            rows[0], rows[1], width, toks, cots,
            lambda j, k=k: blocks[k, 0, pl.ds(j * width, width), :],
            lambda j, k=k: blocks[k, 1, pl.ds(j * width, width), :],
            sums[:parts], sums[parts:],
        )
    for total, out in zip(sums, rounded):
        out[...] = total[...].astype(out.dtype)


def run_pairs(pos, fed, items, spans, accs, rounds, sizes, direct=False):
    slots, width = sizes
    parts, n = len(spans), len(items)
    starts = accs is None
    model = fed[0].shape[1]
    plan = dict(
        pairs=[(len(first), len(second)) for first, second in items],
        spans=spans, starts=starts, rounds=rounds, slots=slots, width=width, direct=direct,
    )
    smem = pl.BlockSpec(memory_space=pltpu.SMEM)
    vmem = pl.BlockSpec(memory_space=pltpu.VMEM)
    hbm = pl.BlockSpec(memory_space=pl.ANY)

    def off_chip(value):
        return pltpu.with_memory_space_constraint(value, pltpu.HBM)

    def on_chip(value):
        return pltpu.with_memory_space_constraint(value, pltpu.VMEM)

    blocks = [on_chip(a) if direct else off_chip(a) for item in items for choice in item for a in choice]
    if starts:
        fed = [off_chip(value) for value in fed]
    operands = [pos, *fed, *blocks, *(accs or [])]
    first_acc = len(operands) - 2 * parts
    out_shape = [jax.ShapeDtypeStruct((size, model), jnp.float32) for _, size in spans] * 2
    if rounds:
        out_shape += [jax.ShapeDtypeStruct((size, model), jnp.bfloat16) for _, size in spans] * 2
    rows = sum(size for _, size in spans)
    scratch = [pltpu.VMEM((n, 2, slots * width + LABEL_ROWS, width), jnp.bfloat16), pltpu.SemaphoreType.DMA((n, 2))]
    if direct:
        scratch = []
    if starts:
        out_shape = [jax.ShapeDtypeStruct((rows, model), jnp.bfloat16)] * 2 + out_shape
        scratch += [pltpu.SemaphoreType.DMA((4,))]
    outs = pl.pallas_call(
        functools.partial(pairs_kernel, plan),
        out_shape=out_shape,
        in_specs=[smem] + [hbm if starts else vmem] * len(fed) + [vmem if direct else hbm] * len(blocks) + [vmem] * len(accs or []),
        out_specs=[vmem] * len(out_shape),
        scratch_shapes=scratch,
        input_output_aliases={} if starts else {first_acc + i: i for i in range(2 * parts)},
        compiler_params=pltpu.CompilerParams(vmem_limit_bytes=PAIRS_VMEM_LIMIT),
        cost_estimate=pl.CostEstimate(
            flops=n * 4 * slots * 2 * rows * width * width,
            transcendentals=n * rows * width,
            bytes_accessed=2 * n * slots * width * width * 2,
        ),
    )(*operands)
    return (outs[:2] if starts else fed), outs[-2 * parts :]


def all_panels_kernel(slots, width, half, meta, tok, cot, held, out, grad, blocks, out_acc, grad_acc, sem):
    def copies(p, buf):
        return [
            pltpu.make_async_copy(held.at[p], blocks.at[buf, 0], sem.at[buf, 0]),
            pltpu.make_async_copy(held.at[half + p], blocks.at[buf, 1], sem.at[buf, 1]),
        ]

    def row_of(r):
        return [meta[r, j] for j in range(slots)], meta[r, slots]

    out_acc[...] = jnp.zeros_like(out_acc)
    grad_acc[...] = jnp.zeros_like(grad_acc)
    for copy in copies(0, 0):
        copy.start()

    def step(p, _):
        buf = lax.rem(p, 2)

        @pl.when(p + 1 < half)
        def _():
            for copy in copies(p + 1, 1 - buf):
                copy.start()

        for copy in copies(p, buf):
            copy.wait()
        run_panel(
            row_of(p), row_of(half + p), width, [tok], [cot],
            lambda j: blocks[buf, 0, j], lambda j: blocks[buf, 1, j], [out_acc], [grad_acc],
        )
        return 0

    lax.fori_loop(0, half, step, 0)
    out[...] = out_acc[...].astype(out.dtype)
    grad[...] = grad_acc[...].astype(grad.dtype)


def run_all(meta, tokens, cotangent, gathered):
    count, slots, width, _ = gathered.shape
    rows, model = tokens.shape
    vmem = pl.BlockSpec(memory_space=pltpu.VMEM)
    return pl.pallas_call(
        functools.partial(all_panels_kernel, slots, width, count // 2),
        out_shape=[jax.ShapeDtypeStruct((rows, model), jnp.bfloat16)] * 2,
        in_specs=[pl.BlockSpec(memory_space=pltpu.SMEM), vmem, vmem, pl.BlockSpec(memory_space=pl.ANY)],
        out_specs=[vmem] * 2,
        scratch_shapes=[
            pltpu.VMEM((2, 2, slots, width, width), jnp.bfloat16),
            pltpu.VMEM((rows, model), jnp.float32),
            pltpu.VMEM((rows, model), jnp.float32),
            pltpu.SemaphoreType.DMA((2, 2)),
        ],
        compiler_params=pltpu.CompilerParams(vmem_limit_bytes=VMEM_LIMIT),
    )(meta, tokens, cotangent, gathered)


def together(*values):
    return lax.optimization_barrier(values)


def after(value, *others):
    return together(value, *others)[0]


def exchange_plan(wide, narrow, slots, blocks):
    return wide == 8 and narrow == 4 and slots <= MOST_SLOTS and blocks <= MOST_BLOCKS


def body(tokens, cotangent, weights, block_index, block_counts):
    wide, narrow = lax.axis_size("wide"), lax.axis_size("narrow")
    slots, width = weights.shape[1], weights.shape[2]
    if not exchange_plan(wide, narrow, slots, tokens.shape[1] // width):
        own_meta = jnp.concatenate([block_index, block_counts[:, None]], axis=1)
        meta = lax.all_gather(own_meta, BOTH, axis=0, tiled=True)
        gathered = lax.all_gather(weights, BOTH, axis=0, tiled=True)
        return tuple(run_all(meta, tokens, cotangent, gathered))

    def across(value, bit):
        return lax.ppermute(value, "wide", [(i, i ^ bit) for i in range(wide)])

    core, x, y = (functools.partial(across, bit=bit) for bit in (1, 2, 4))

    def line(value, pairs):
        return lax.ppermute(value, "narrow", pairs)

    w, z = lax.axis_index("wide"), lax.axis_index("narrow")
    pos = jnp.stack([(w < wide // 2).astype(jnp.int32), z.astype(jnp.int32)])
    mid = (z == 1) | (z == 2)
    run = functools.partial(run_pairs, sizes=(slots, width))
    rows = tokens.shape[0]
    mine, others = (0, rows), (rows, rows)

    own = with_labels(weights, block_index, block_counts)
    near, x_own, beyond, y_own = line(own, ENDS), x(own), line(own, MIDDLE), y(own)
    near, x_own, beyond, y_own = together(near, x_own, beyond, y_own)
    both = jnp.concatenate([tokens, cotangent], axis=0)

    out1, in1 = line(beyond, OUTWARD), line(near, MIDDLE)
    y_near, xy_own = y(after(near, y_own)), x(after(y_own, x_own))
    both_other = core(after(both, x_own))

    out2, xy_beyond = line(after(in1, out1), OUTWARD), line(after(xy_own, in1), MIDDLE)
    third = jnp.where(mid, beyond, out1)
    y_third, x_near = y(after(third, y_near)), x(after(near, xy_own))

    last = jnp.where(mid, in1, out2)
    x_last, xy_near, y_last = x(after(last, x_near)), line(after(xy_own, out2), ENDS), y(after(last, y_third))
    fed, accs = run(pos, [tokens, cotangent, both_other], [
        ([own], [y_own]), ([near], [y_near]), ([x_own], [xy_own]),
    ], [mine, others], None, False)

    xy_last, x_third, out3 = y(after(x_last, y_last)), x(after(third, x_last)), line(after(xy_beyond, xy_near), OUTWARD)
    fed, accs = run(pos, fed, [
        ([beyond, out1], [y_third]), ([x_near], [xy_near]), ([in1, out2], [y_last]),
    ], [mine, others], accs, False)

    ending = [([x_last], [xy_last]), ([x_third], [xy_beyond, out3])]
    _, sent = run(pos, fed, ending, [others], [accs[1], accs[3]], True, direct=True)
    got = [core(part) for part in sent]
    _, kept = run(pos, fed, ending, [mine], [accs[0], accs[2]], False, direct=True)
    return tuple(add_rounded(kept, got))


def solution(mesh):
    rows = P(BOTH, None)
    return jax.shard_map(
        body,
        mesh=mesh,
        in_specs=(rows, rows, P(BOTH, None, None, None), rows, P(BOTH)),
        out_specs=(rows, rows),
        check_vma=False,
    )
```
